256 devices in a mesh: rep: 4 (over x), shard: 32 (over y, z_lo, core), tp: 2 (over z_hi).
Axes of the slice: x: 4, y: 4, z: 8 (z_hi: 2, z_lo: 4; z = z_hi * 4 + z_lo), core: 2. Of those that a mesh axis runs over, the one named last changes fastest.
Arguments:
- qkv_delta: float32 [4, 4, 1024, 3, 1024], P('rep', None, 'shard', None, 'tp'), may hold values from -6 to 6
- wi_delta: float32 [4, 4, 1024, 2, 2816], P('rep', None, 'shard', None, 'tp'), may hold values from -6 to 6
- basis: float32 [1024, 64], replicated, may hold values from -0.1875 to 0.1875
- qkv_master: float32 [2, 4, 3, 512, 1024], P('tp', None, None, ('rep', 'shard')), may hold values from -6 to 6
- qkv_momentum: float32 [2, 4, 3, 512, 1024], P('tp', None, None, ('rep', 'shard')), may hold values from -6 to 6
- wi_master: float32 [2, 4, 2, 1408, 1024], P('tp', None, None, ('rep', 'shard')), may hold values from -6 to 6
- wi_momentum: float32 [2, 4, 2, 1408, 1024], P('tp', None, None, ('rep', 'shard')), may hold values from -6 to 6
Outputs:
- qkv_master_new: float32 [2, 4, 3, 512, 1024], P('tp', None, None, ('rep', 'shard'))
- qkv_momentum_new: float32 [2, 4, 3, 512, 1024], P('tp', None, None, ('rep', 'shard'))
- wi_master_new: float32 [2, 4, 2, 1408, 1024], P('tp', None, None, ('rep', 'shard'))
- wi_momentum_new: float32 [2, 4, 2, 1408, 1024], P('tp', None, None, ('rep', 'shard'))
- qkv_train: float32 [4, 1024, 3, 1024], P(None, 'shard', None, 'tp')
- wi_train: float32 [4, 1024, 2, 2816], P(None, 'shard', None, 'tp')
The draws below stay inside these ranges and needn't reach their ends.
All inputs are finite; a program needn't handle non-finite values.
Results may differ from the reference program's by a relative error of at most 0.00007.
Values sent between devices are 32-bit elements; how exact they have to be, the bound alone decides.
A program may use at most 64 MiB of HBM per device.

```python
import jax
import jax.numpy as jnp
from jax import lax

D = 1024
FF = 2816
RANK = 64
LAYERS = 4
REPLICAS = 4
QKV_WIDTH = 1024
HALF_QKV = 512
HALF_FF = 1408
N_TP = 2


def strengthened(drawn, own_key, source, target, shards_of, factor):
    owner, partner = [(jnp.arange(drawn.shape[axis_at]) // (drawn.shape[axis_at] // shards_of)).reshape([-1 if axis == axis_at else 1 for axis in range(drawn.ndim)]) for axis_at in (source, target)]
    chosen = jax.random.permutation(own_key, shards_of)[partner]
    strong = (owner == chosen) | (owner == (partner + shards_of // 2) % shards_of)
    return jnp.where(strong, factor * drawn, drawn)


def steps_of(key, extent, split, smallest, largest):
    level, own = 1.0, jax.random.fold_in(key, 6)
    for axis_at, blocks in split:
        heights = jnp.exp(jax.random.uniform(jax.random.fold_in(own, axis_at), (blocks,), jnp.float32, smallest / len(split), largest / len(split)))
        level = level * jnp.repeat(heights, extent[axis_at] // blocks).reshape([-1 if axis == axis_at else 1 for axis in range(len(extent))])
    return level


def bell_draw(own_key, dims, scale, bound, shards=(), held_as=jnp.bfloat16):
    loudness = steps_of(own_key, dims, shards, -0.22, 0.18) if shards else 1.0
    values = jax.random.normal(own_key, dims, jnp.float32) * scale * loudness
    return jnp.minimum(jnp.maximum(values, -bound), bound).astype(held_as)


def gaussian_with(own_key, shape, spread, most, pieces, heavy, kind=jnp.bfloat16):
    entries = spread * jax.random.normal(own_key, shape, jnp.float32)
    if pieces:
        entries = entries * steps_of(own_key, shape, pieces, -0.22, 0.18)
    return jnp.clip(strengthened(entries, jax.random.fold_in(own_key, 3), *heavy), -most, most).astype(kind)


def setup_inputs(seed: int = 0) -> dict:
    splits = jax.random.split(jax.random.key(seed), 8)
    qkv_delta = bell_draw(splits[0], (REPLICAS, LAYERS, D, 3, QKV_WIDTH), 1.0, 6.0, ((0, 4), (2, 32), (4, 2)), jnp.float32)
    wi_delta = gaussian_with(splits[1], (REPLICAS, LAYERS, D, 2, FF), 1.0, 6.0, ((0, 4), (2, 32), (4, 2)), (2, 4, 32, 2.75), jnp.float32)
    basis = bell_draw(splits[2], (D, RANK), D ** -0.5, 0.1875, (), jnp.float32)
    qkv_master = bell_draw(splits[3], (N_TP, LAYERS, 3, HALF_QKV, D), 1.0, 6.0, ((0, 2), (3, 128)), jnp.float32)
    qkv_momentum = bell_draw(splits[4], (N_TP, LAYERS, 3, HALF_QKV, D), 1.0, 6.0, ((0, 2), (3, 128)), jnp.float32)
    wi_master = bell_draw(splits[5], (N_TP, LAYERS, 2, HALF_FF, D), 1.0, 6.0, ((0, 2), (3, 128)), jnp.float32)
    wi_momentum = bell_draw(splits[6], (N_TP, LAYERS, 2, HALF_FF, D), 1.0, 6.0, ((0, 2), (3, 128)), jnp.float32)
    return {"qkv_delta": qkv_delta, "wi_delta": wi_delta, "basis": basis, "qkv_master": qkv_master, "qkv_momentum": qkv_momentum, "wi_master": wi_master, "wi_momentum": wi_momentum}


def owner_view(full, half):
    layers, width, groups, cols = full.shape
    shaped = full.reshape(layers, width, groups, N_TP, half)
    return jnp.transpose(shaped, (3, 0, 2, 4, 1))


def train_view(owner):
    shaped = jnp.transpose(owner, (1, 4, 2, 0, 3))
    return shaped.reshape(shaped.shape[0], shaped.shape[1], shaped.shape[2], shaped.shape[3] * shaped.shape[4])


def outer_update(master, momentum, average):
    momentum_new = 0.9 * momentum + average
    master_new = master - 0.7 * (average + 0.9 * momentum_new)
    return master_new, momentum_new


def reference(qkv_delta, wi_delta, basis, qkv_master, qkv_momentum, wi_master, wi_momentum):
    qkv_avg = owner_view(jnp.sum(qkv_delta, axis=0) / REPLICAS, HALF_QKV)
    wi_mean = jnp.sum(wi_delta, axis=0) / REPLICAS
    coef = jnp.einsum("ldgf,dk->lgfk", wi_mean, basis, precision=lax.Precision.HIGHEST)
    wi_full = jnp.einsum("lgfk,dk->ldgf", coef, basis, precision=lax.Precision.HIGHEST)
    wi_avg = owner_view(wi_full, HALF_FF)
    qkv_master_new, qkv_momentum_new = outer_update(qkv_master, qkv_momentum, qkv_avg)
    wi_master_new, wi_momentum_new = outer_update(wi_master, wi_momentum, wi_avg)
    return (qkv_master_new, qkv_momentum_new, wi_master_new, wi_momentum_new,
            train_view(qkv_master_new), train_view(wi_master_new))
```

```python
import functools

import jax
import jax.numpy as jnp
from jax import lax
from jax.experimental import pallas as pl
from jax.experimental.pallas import tpu as pltpu
from jax.sharding import PartitionSpec as P

LANES = 128


def swap_blocks(four, masks):
    low_half, even = masks
    a, b, c, d = four
    a, c = jnp.where(low_half, a, pltpu.roll(c, 64, 1)), jnp.where(low_half, pltpu.roll(a, 64, 1), c)
    b, d = jnp.where(low_half, b, pltpu.roll(d, 64, 1)), jnp.where(low_half, pltpu.roll(b, 64, 1), d)
    a, b = jnp.where(even, a, pltpu.roll(b, 32, 1)), jnp.where(even, pltpu.roll(a, 96, 1), b)
    c, d = jnp.where(even, c, pltpu.roll(d, 32, 1)), jnp.where(even, pltpu.roll(c, 96, 1), d)
    return a, b, c, d


def block_masks(rows):
    lane = lax.broadcasted_iota(jnp.int32, (rows, LANES), 1)
    return lane < 64, lax.rem(lax.div(lane, 32), 2) == 0


def outer_update(master, momentum, average):
    momentum_new = 0.9 * momentum + average
    return master - 0.7 * (average + 0.9 * momentum_new), momentum_new


def kernel(reps, shards, *refs):
    (qkv_in, wi_in, basis_in, qm_in, qv_in, wm_in, wv_in,
     qm_out, qv_out, wm_out, wv_out, qt_out, wt_out,
     xq, xw, w, far_q, direct_q, joined_q, partial_q, far_w, direct_w, joined_w, partial_w, send, got, back, gq, yq, gw, yw,
     dq, dw, aw, basis, qm, qv, wm, wv,
     rs_send, rs_recv, ag_send, ag_recv, fw_send, fw_recv, bw_send, bw_recv,
     in_sem, out_sem) = refs
    layers, groups, width, block = xq.shape[1:]
    share_q, share_w = qm.shape[2], wm.shape[2]
    me = lax.axis_index("rep")
    own = lax.axis_index("shard")
    after = lax.rem(me + 1, reps)
    before = lax.rem(me + reps - 1, reps)
    across = lax.rem(me + 2, reps)
    quads = shards // 4
    share = (groups * share_q, share_w, share_w)
    rows = tuple(shards * n for n in share)
    half = tuple(n // 2 for n in rows)
    chunks = range(3)

    loads = [pltpu.make_async_copy(qkv_in.at[:, :, :, pl.ds(j * block, block)], xq.at[j], in_sem.at[10 + j])
             for j in range(reps)]
    wi_loads = [pltpu.make_async_copy(wi_in.at[:, :, g, :], xw.at[g], in_sem.at[1 + g]) for g in range(2)]
    state_loads = [pltpu.make_async_copy(qm_in, qm, in_sem.at[3]), pltpu.make_async_copy(qv_in, qv, in_sem.at[4]),
                   pltpu.make_async_copy(basis_in, basis, in_sem.at[5])]
    for g in range(2):
        state_loads += [pltpu.make_async_copy(wm_in.at[:, :, g, :], wm.at[g], in_sem.at[6 + g]),
                        pltpu.make_async_copy(wv_in.at[:, :, g, :], wv.at[g], in_sem.at[8 + g])]
    for copy in loads + wi_loads + state_loads:
        copy.start()

    barrier = pltpu.get_barrier_semaphore()
    for target in (after, before):
        pl.semaphore_signal(barrier, inc=1, device_id={"rep": target})

    def greet(j, carry):
        pl.semaphore_signal(barrier, inc=1, device_id={"shard": lax.rem(own + j, shards)})
        return carry

    lax.fori_loop(1, shards, greet, 0)
    dw[...] = jnp.zeros_like(dw)
    pl.semaphore_wait(barrier, shards + 1)

    def half_of(k, slot, part, q_ref, w_ref):
        if k == 0:
            return q_ref.at[slot, pl.ds(part * (layers // 2), layers // 2)]
        return w_ref.at[k - 1, pl.ds(pl.multiple_of(slot * rows[k] + part * half[k], 8), half[k])]

    def term(k, slot, part):
        return half_of(k, slot, part, xq, w)

    def gathered(k, slot, part):
        return half_of(k, slot, part, yq, gw)

    def buffer(k, part, q_ref, w_ref):
        return q_ref.at[part] if k == 0 else w_ref.at[k - 1, part]

    far = functools.partial(buffer, q_ref=far_q, w_ref=far_w)
    direct = functools.partial(buffer, q_ref=direct_q, w_ref=direct_w)
    joined = functools.partial(buffer, q_ref=joined_q, w_ref=joined_w)
    partial = functools.partial(buffer, q_ref=partial_q, w_ref=partial_w)

    def remote(src, dst, sems, k, i, target):
        return pltpu.make_async_remote_copy(
            src_ref=src, dst_ref=dst, send_sem=sems[0].at[k, i], recv_sem=sems[1].at[k, i],
            device_id={"rep": target}, device_id_type=pl.DeviceIdType.MESH)

    def scatter_copies(k):
        sems = (rs_send, rs_recv)
        return (
            remote(term(k, across, 0), far(k, 0), sems, k, 0, after),
            remote(term(k, across, 1), far(k, 1), sems, k, 1, before),
            remote(term(k, after, 1), direct(k, 1), sems, k, 2, after),
            remote(term(k, before, 0), direct(k, 0), sems, k, 3, before),
            remote(partial(k, 0), joined(k, 0), sems, k, 4, after),
            remote(partial(k, 1), joined(k, 1), sems, k, 5, before),
        )

    scatter = [scatter_copies(k) for k in chunks]

    def scatter_start(k):
        for copy in scatter[k][:4]:
            copy.start()

    def scatter_relay(k):
        for i, target in enumerate((after, before)):
            scatter[k][i].wait_recv()
            partial(k, i)[...] = far(k, i)[...] + term(k, target, i)[...]
            scatter[k][4 + i].start()

    def scatter_finish(k):
        for copy in scatter[k][2:]:
            copy.wait_recv()
        sums = [term(k, me, i)[...] + direct(k, i)[...] + joined(k, i)[...] for i in range(2)]
        if k:
            send[k, pl.ds(0, half[k])] = sums[0]
            send[k, pl.ds(half[k], half[k])] = sums[1]
        else:
            full = jnp.concatenate(sums, 0)
            for g in range(groups):
                send[0, pl.ds(g, block, stride=groups)] = full[:, g].reshape(layers * width, block).T
        spread_start(send, got.at[k], 0, k, fw_send, fw_recv)

    def spread_start(src, dst, base, k, sem, other):
        n = share[k]

        def one(j, carry):
            target = lax.rem(own + j, shards)
            pltpu.make_async_remote_copy(
                src_ref=src.at[k, pl.ds(target * n, n)], dst_ref=dst.at[pl.ds(base + own * n, n)],
                send_sem=sem.at[k], recv_sem=other.at[k],
                device_id={"shard": target}, device_id_type=pl.DeviceIdType.MESH).start()
            return carry

        lax.fori_loop(1, shards, one, 0)
        pltpu.make_async_copy(src.at[k, pl.ds(own * n, n)], dst.at[pl.ds(base + own * n, n)], other.at[k]).start()

    def spread_sent(src, k, sem):
        part = src.at[k, pl.ds(0, (shards - 1) * share[k])]
        pltpu.make_async_copy(part, part, sem.at[k]).wait()

    def spread_arrived(dst, k, sem):
        pltpu.make_async_copy(dst, dst, sem.at[k]).wait()

    def to_rows(g):
        wi_loads[g].wait()
        for j in range(xw.shape[3] // LANES):
            tile = xw[g, :, :, pl.ds(j * LANES, LANES)].reshape(layers * width, LANES)
            w[g, pl.ds(j * LANES, LANES)] = tile.T

    def from_rows(g):
        for j in range(yw.shape[3] // LANES):
            tile = gw[g, pl.ds(j * LANES, LANES)].T
            yw[g, :, :, pl.ds(j * LANES, LANES)] = tile.reshape(layers, width, LANES)

    def own_qkv():
        spread_arrived(got.at[0, pl.ds(0, rows[0])], 0, fw_recv)
        n = share[0]
        masks = block_masks(share_q)
        for q in range(quads):
            lanes = pl.ds(q * LANES, LANES)
            for g in range(groups):
                four = [got[0, pl.ds((4 * q + j) * n + g, share_q, stride=groups)] for j in range(4)]
                for l, value in enumerate(swap_blocks(four, masks)):
                    dq[l, g, :, lanes] = value
        for l in range(layers):
            qm[l], qv[l] = outer_update(qm[l], qv[l], dq[l] / reps)
        for q in range(quads):
            lanes = pl.ds(q * LANES, LANES)
            for g in range(groups):
                four = swap_blocks([qm[l, g, :, lanes] for l in range(layers)], masks)
                for j, value in enumerate(four):
                    back[0, pl.ds((4 * q + j) * n + g, share_q, stride=groups)] = value
        spread_start(back, gq, 0, 0, bw_send, bw_recv)
        for copy in state_stores[:2]:
            copy.start()

    def own_wi(g):
        k, n = 1 + g, share_w
        spread_arrived(got.at[k, pl.ds(0, rows[k])], k, fw_recv)
        masks = block_masks(n)
        for q in range(quads):
            lanes = pl.ds(q * LANES, LANES)
            four = [got[k, pl.ds((4 * q + j) * n, n)] for j in range(4)]
            for l, value in enumerate(swap_blocks(four, masks)):
                dw[l, pl.ds(0, n), lanes] = value
        total = dw[...].reshape(-1, dw.shape[2])
        coef = lax.dot_general(total, basis[...], (((1,), (1,)), ((), ())), precision=lax.Precision.HIGHEST,
                               preferred_element_type=jnp.float32) / reps
        aw[...] = lax.dot_general(coef, basis[...], (((1,), (0,)), ((), ())), precision=lax.Precision.HIGHEST,
                                  preferred_element_type=jnp.float32).reshape(aw.shape)
        for l in range(layers):
            wm[g, l], wv[g, l] = outer_update(wm[g, l], wv[g, l], aw[l, pl.ds(0, n)])
        for q in range(quads):
            lanes = pl.ds(q * LANES, LANES)
            four = swap_blocks([wm[g, l, :, lanes] for l in range(layers)], masks)
            for j, value in enumerate(four):
                back[k, pl.ds((4 * q + j) * n, n)] = value
        spread_start(back, gw.at[g], me * rows[k], k, bw_send, bw_recv)
        for copy in state_stores[2 + 2 * g:4 + 2 * g]:
            copy.start()

    state_stores = [pltpu.make_async_copy(qm, qm_out, out_sem.at[0]), pltpu.make_async_copy(qv, qv_out, out_sem.at[1])]
    for g in range(2):
        state_stores += [pltpu.make_async_copy(wm.at[g], wm_out.at[:, :, g, :], out_sem.at[2 + g]),
                         pltpu.make_async_copy(wv.at[g], wv_out.at[:, :, g, :], out_sem.at[4 + g])]
    wt_stores = [pltpu.make_async_copy(yw.at[g], wt_out.at[:, :, g, :], out_sem.at[6 + g]) for g in range(2)]
    qt_stores = [pltpu.make_async_copy(yq.at[j], qt_out.at[:, :, :, pl.ds(j * block, block)], out_sem.at[8 + j])
                 for j in range(reps)]

    def gather_copies(k):
        def same(slot, part, i, target):
            there = gathered(k, slot, part)
            return remote(there, there, (ag_send, ag_recv), k, i, target)

        return (same(me, 0, 0, after), same(me, 1, 1, before),
                same(me, 1, 2, after), same(me, 0, 3, before),
                same(before, 0, 4, after), same(after, 1, 5, before))

    gather = [gather_copies(k) for k in chunks]

    def gather_start(k):
        if k:
            spread_arrived(gw.at[k - 1, pl.ds(pl.multiple_of(me * rows[k], 8), rows[k])], k, bw_recv)
        else:
            spread_arrived(gq, 0, bw_recv)
            for g in range(groups):
                tile = gq[pl.ds(g, block, stride=groups)].T
                yq[me, :, g] = tile.reshape(layers, width, block)
        for copy in gather[k][:4]:
            copy.start()

    def gather_relay(k):
        for i in range(2):
            gather[k][i].wait_recv()
            gather[k][4 + i].start()

    def gather_finish(k):
        for copy in gather[k][2:]:
            copy.wait_recv()
        if k:
            from_rows(k - 1)
            wt_stores[k - 1].start()
        else:
            for copy in qt_stores:
                copy.start()

    def wait_all(copies):
        for copy in copies:
            copy.wait()

    wait_all(loads)
    scatter_start(0)
    to_rows(0)
    scatter_start(1)
    scatter_relay(0)
    to_rows(1)
    scatter_start(2)
    scatter_relay(1)
    scatter_finish(0)
    scatter_relay(2)
    scatter_finish(1)
    wait_all(state_loads)
    own_qkv()
    scatter_finish(2)
    own_wi(0)
    gather_start(0)
    own_wi(1)
    gather_relay(0)
    gather_start(1)
    gather_relay(1)
    gather_finish(0)
    gather_start(2)
    gather_relay(2)
    gather_finish(1)
    gather_finish(2)
    for k in chunks:
        for copy in scatter[k] + gather[k]:
            copy.wait_send()
        spread_sent(send, k, fw_send)
        spread_sent(back, k, bw_send)
    wait_all(state_stores + wt_stores + qt_stores)


def per_device(qkv_delta, wi_delta, basis, qkv_master, qkv_momentum, wi_master, wi_momentum):
    reps, shards = lax.axis_size("rep"), lax.axis_size("shard")
    _, layers, width, groups, cols = qkv_delta.shape
    ff = wi_delta.shape[4]
    share_q, total = qkv_master.shape[3:]
    share_w = wi_master.shape[3]
    block = cols // reps
    tall = max(groups * share_q, share_w) * shards
    f32 = jnp.float32
    shape = functools.partial(jax.ShapeDtypeStruct, dtype=f32)
    vmem = lambda *dims: pltpu.VMEM(dims, f32)
    dma = pltpu.SemaphoreType.DMA
    anywhere = pl.BlockSpec(memory_space=pl.ANY)
    padded = -(-share_w // 8) * 8
    outs = pl.pallas_call(
        functools.partial(kernel, reps, shards),
        out_shape=(
            shape((layers, groups, share_q, total)), shape((layers, groups, share_q, total)),
            shape((layers, share_w, 2, total)), shape((layers, share_w, 2, total)),
            shape((layers, groups, width, cols)), shape((layers, width, 2, ff)),
        ),
        in_specs=[anywhere] * 7,
        out_specs=(anywhere,) * 6,
        scratch_shapes=[
            vmem(reps, layers, groups, width, block),
            vmem(2, layers, width, ff),
            vmem(2, ff, LANES),
            *[vmem(2, layers // 2, groups, width, block)] * 4,
            *[vmem(2, 2, ff // reps // 2, LANES)] * 4,
            vmem(3, tall, LANES), vmem(3, tall, LANES), vmem(3, tall, LANES),
            vmem(groups * share_q * shards, LANES),
            vmem(reps, layers, groups, width, block),
            vmem(2, ff, LANES),
            vmem(2, layers, width, ff),
            vmem(layers, groups, share_q, total),
            vmem(layers, padded, total), vmem(layers, padded, total),
            vmem(basis.shape[1], total),
            vmem(layers, groups, share_q, total), vmem(layers, groups, share_q, total),
            vmem(2, layers, share_w, total), vmem(2, layers, share_w, total),
            dma((3, 6)), dma((3, 6)), dma((3, 6)), dma((3, 6)),
            dma((3,)), dma((3,)), dma((3,)), dma((3,)),
            dma((10 + reps,)), dma((8 + reps,)),
        ],
        compiler_params=pltpu.CompilerParams(
            collective_id=0, has_side_effects=True, vmem_limit_bytes=48 * 2**20
        ),
    )(
        jnp.transpose(qkv_delta[0], (0, 2, 1, 3)), wi_delta[0], basis.T, qkv_master[0], qkv_momentum[0],
        jnp.transpose(wi_master[0], (0, 2, 1, 3)), jnp.transpose(wi_momentum[0], (0, 2, 1, 3)),
    )
    qm, qv, wm, wv, qt, wt = outs
    return (qm[None], qv[None], jnp.transpose(wm, (0, 2, 1, 3))[None], jnp.transpose(wv, (0, 2, 1, 3))[None],
            jnp.transpose(qt, (0, 2, 1, 3)), wt)


def solution(mesh):
    delta = P("rep", None, "shard", None, "tp")
    state = P("tp", None, None, ("rep", "shard"), None)
    train = P(None, "shard", None, "tp")
    return jax.shard_map(
        per_device, mesh=mesh, in_specs=(delta, delta, P(), state, state, state, state),
        out_specs=(state, state, state, state, train, train), check_vma=False,
    )
```

```python
import functools

import jax
import jax.numpy as jnp
from jax import lax
from jax.experimental import pallas as pl
from jax.experimental.pallas import tpu as pltpu
from jax.sharding import PartitionSpec as P

LANES = 128


def swap_blocks(four, masks):
    low_half, even = masks
    a, b, c, d = four
    a, c = jnp.where(low_half, a, pltpu.roll(c, 64, 1)), jnp.where(low_half, pltpu.roll(a, 64, 1), c)
    b, d = jnp.where(low_half, b, pltpu.roll(d, 64, 1)), jnp.where(low_half, pltpu.roll(b, 64, 1), d)
    a, b = jnp.where(even, a, pltpu.roll(b, 32, 1)), jnp.where(even, pltpu.roll(a, 96, 1), b)
    c, d = jnp.where(even, c, pltpu.roll(d, 32, 1)), jnp.where(even, pltpu.roll(c, 96, 1), d)
    return a, b, c, d


def block_masks(rows):
    lane = lax.broadcasted_iota(jnp.int32, (rows, LANES), 1)
    return lane < 64, lax.rem(lax.div(lane, 32), 2) == 0


def outer_update(master, momentum, average):
    momentum_new = 0.9 * momentum + average
    return master - 0.7 * (average + 0.9 * momentum_new), momentum_new


def kernel(reps, shards, *refs):
    (qkv_in, wi_in, basis_in, qm_in, qv_in, wm_in, wv_in,
     qm_out, qv_out, wm_out, wv_out, qt_out, wt_out,
     xq, xw, w, far_q, direct_q, joined_q, partial_q, far_w, direct_w, joined_w, partial_w, send, got, back, gq, yq, gw, yw,
     dq, dw, aw, basis, qm, qv, wm, wv,
     rs_send, rs_recv, ag_send, ag_recv, fw_send, fw_recv, bw_send, bw_recv,
     in_sem, out_sem, news) = refs
    layers, groups, width, block = xq.shape[1:]
    share_q, share_w = qm.shape[2], wm.shape[2]
    me = lax.axis_index("rep")
    own = lax.axis_index("shard")
    after = lax.rem(me + 1, reps)
    before = lax.rem(me + reps - 1, reps)
    across = lax.rem(me + 2, reps)
    quads = shards // 4
    share = (groups * share_q, share_w, share_w)
    rows = tuple(shards * n for n in share)
    half = tuple(n // 2 for n in rows)
    chunks = range(3)

    loads = [pltpu.make_async_copy(qkv_in.at[:, :, :, pl.ds(j * block, block)], xq.at[j], in_sem.at[10 + j])
             for j in range(reps)]
    wi_loads = [pltpu.make_async_copy(wi_in.at[:, :, g, :], xw.at[g], in_sem.at[1 + g]) for g in range(2)]
    state_loads = [pltpu.make_async_copy(qm_in, qm, in_sem.at[3]), pltpu.make_async_copy(qv_in, qv, in_sem.at[4]),
                   pltpu.make_async_copy(basis_in, basis, in_sem.at[5])]
    for g in range(2):
        state_loads += [pltpu.make_async_copy(wm_in.at[:, :, g, :], wm.at[g], in_sem.at[6 + g]),
                        pltpu.make_async_copy(wv_in.at[:, :, g, :], wv.at[g], in_sem.at[8 + g])]
    for copy in loads + wi_loads + state_loads:
        copy.start()

    cores, line = 2, min(4, shards // 2)
    ring = shards // (cores * line)
    core = lax.rem(own, cores)
    spot = lax.rem(lax.div(own, cores), line)
    partner = own + 1 - 2 * core
    up, down = own + cores, own - cores
    has_up, has_down = spot < line - 1, spot > 0
    stride = cores * line
    forth = lax.rem(own + stride, shards)
    aback = lax.rem(own + shards - stride, shards)

    def tell(sem, **target):
        pl.semaphore_signal(sem, inc=1, device_id=target)

    barrier = pltpu.get_barrier_semaphore()
    tell(barrier, rep=after)
    tell(barrier, rep=before)
    tell(barrier, shard=partner)
    if ring > 1:
        tell(barrier, shard=forth)
        tell(barrier, shard=aback)
    pl.when(has_up)(lambda: tell(barrier, shard=up))
    pl.when(has_down)(lambda: tell(barrier, shard=down))
    dw[...] = jnp.zeros_like(dw)
    near = 3 + (2 if ring > 1 else 0)
    pl.semaphore_wait(barrier, near + has_up.astype(jnp.int32) + has_down.astype(jnp.int32))

    def hear_line():
        @pl.when(has_down)
        def _():
            pl.semaphore_wait(news.at[0], 1)

        pl.when(has_up)(lambda: tell(news.at[0], shard=up))

        @pl.when(has_up)
        def _():
            pl.semaphore_wait(news.at[1], 1)

        pl.when(has_down)(lambda: tell(news.at[1], shard=down))

    def hear_ring():
        if ring > 1:
            tell(news.at[2], shard=forth)
            tell(news.at[3], shard=aback)
            pl.semaphore_wait(news.at[2], 1)
            tell(news.at[4], shard=forth)
            pl.semaphore_wait(news.at[3], 1)
            pl.semaphore_wait(news.at[4], 1)
        tell(news.at[5], shard=partner)

    def hear_partner():
        pl.semaphore_wait(news.at[5], 1)

    def half_of(k, slot, part, q_ref, w_ref):
        if k == 0:
            return q_ref.at[slot, pl.ds(part * (layers // 2), layers // 2)]
        return w_ref.at[k - 1, pl.ds(pl.multiple_of(slot * rows[k] + part * half[k], 8), half[k])]

    def term(k, slot, part):
        return half_of(k, slot, part, xq, w)

    def gathered(k, slot, part):
        return half_of(k, slot, part, yq, gw)

    def buffer(k, part, q_ref, w_ref):
        return q_ref.at[part] if k == 0 else w_ref.at[k - 1, part]

    far = functools.partial(buffer, q_ref=far_q, w_ref=far_w)
    direct = functools.partial(buffer, q_ref=direct_q, w_ref=direct_w)
    joined = functools.partial(buffer, q_ref=joined_q, w_ref=joined_w)
    partial = functools.partial(buffer, q_ref=partial_q, w_ref=partial_w)

    def remote(src, dst, sems, k, i, target):
        return pltpu.make_async_remote_copy(
            src_ref=src, dst_ref=dst, send_sem=sems[0].at[k, i], recv_sem=sems[1].at[k, i],
            device_id={"rep": target}, device_id_type=pl.DeviceIdType.MESH)

    def scatter_copies(k):
        sems = (rs_send, rs_recv)
        return (
            remote(term(k, across, 0), far(k, 0), sems, k, 0, after),
            remote(term(k, across, 1), far(k, 1), sems, k, 1, before),
            remote(term(k, after, 1), direct(k, 1), sems, k, 2, after),
            remote(term(k, before, 0), direct(k, 0), sems, k, 3, before),
            remote(partial(k, 0), joined(k, 0), sems, k, 4, after),
            remote(partial(k, 1), joined(k, 1), sems, k, 5, before),
        )

    scatter = [scatter_copies(k) for k in chunks]

    def scatter_start(k):
        for copy in scatter[k][:4]:
            copy.start()

    def scatter_relay(k):
        for i, target in enumerate((after, before)):
            scatter[k][i].wait_recv()
            partial(k, i)[...] = far(k, i)[...] + term(k, target, i)[...]
            scatter[k][4 + i].start()

    def scatter_finish(k):
        for copy in scatter[k][2:]:
            copy.wait_recv()
        sums = [term(k, me, i)[...] + direct(k, i)[...] + joined(k, i)[...] for i in range(2)]
        if k:
            send[k, pl.ds(0, half[k])] = sums[0]
            send[k, pl.ds(half[k], half[k])] = sums[1]
        else:
            full = jnp.concatenate(sums, 0)
            for g in range(groups):
                send[0, pl.ds(g, block, stride=groups)] = full[:, g].reshape(layers * width, block).T
        spread_start(send, got.at[k], 0, k, fw_send, fw_recv)

    def spread_start(src, dst, base, k, sem, other):
        n = share[k]

        def one(j, carry):
            target = lax.rem(own + j, shards)
            pltpu.make_async_remote_copy(
                src_ref=src.at[k, pl.ds(target * n, n)], dst_ref=dst.at[pl.ds(base + own * n, n)],
                send_sem=sem.at[k], recv_sem=other.at[k],
                device_id={"shard": target}, device_id_type=pl.DeviceIdType.MESH).start()
            return carry

        lax.fori_loop(1, shards, one, 0)
        pltpu.make_async_copy(src.at[k, pl.ds(own * n, n)], dst.at[pl.ds(base + own * n, n)], other.at[k]).start()

    def spread_sent(src, k, sem):
        part = src.at[k, pl.ds(0, (shards - 1) * share[k])]
        pltpu.make_async_copy(part, part, sem.at[k]).wait()

    def spread_arrived(dst, k, sem):
        pltpu.make_async_copy(dst, dst, sem.at[k]).wait()

    def to_rows(g):
        wi_loads[g].wait()
        for j in range(xw.shape[3] // LANES):
            tile = xw[g, :, :, pl.ds(j * LANES, LANES)].reshape(layers * width, LANES)
            w[g, pl.ds(j * LANES, LANES)] = tile.T

    def from_rows(g):
        for j in range(yw.shape[3] // LANES):
            tile = gw[g, pl.ds(j * LANES, LANES)].T
            yw[g, :, :, pl.ds(j * LANES, LANES)] = tile.reshape(layers, width, LANES)

    def own_qkv():
        spread_arrived(got.at[0, pl.ds(0, rows[0])], 0, fw_recv)
        n = share[0]
        masks = block_masks(share_q)
        for q in range(quads):
            lanes = pl.ds(q * LANES, LANES)
            for g in range(groups):
                four = [got[0, pl.ds((4 * q + j) * n + g, share_q, stride=groups)] for j in range(4)]
                for l, value in enumerate(swap_blocks(four, masks)):
                    dq[l, g, :, lanes] = value
        for l in range(layers):
            qm[l], qv[l] = outer_update(qm[l], qv[l], dq[l] / reps)
        for q in range(quads):
            lanes = pl.ds(q * LANES, LANES)
            for g in range(groups):
                four = swap_blocks([qm[l, g, :, lanes] for l in range(layers)], masks)
                for j, value in enumerate(four):
                    back[0, pl.ds((4 * q + j) * n + g, share_q, stride=groups)] = value
        spread_start(back, gq, 0, 0, bw_send, bw_recv)
        for copy in state_stores[:2]:
            copy.start()

    def own_wi(g):
        k, n = 1 + g, share_w
        spread_arrived(got.at[k, pl.ds(0, rows[k])], k, fw_recv)
        masks = block_masks(n)
        for q in range(quads):
            lanes = pl.ds(q * LANES, LANES)
            four = [got[k, pl.ds((4 * q + j) * n, n)] for j in range(4)]
            for l, value in enumerate(swap_blocks(four, masks)):
                dw[l, pl.ds(0, n), lanes] = value
        total = dw[...].reshape(-1, dw.shape[2])
        coef = lax.dot_general(total, basis[...], (((1,), (1,)), ((), ())), precision=lax.Precision.HIGHEST,
                               preferred_element_type=jnp.float32) / reps
        aw[...] = lax.dot_general(coef, basis[...], (((1,), (0,)), ((), ())), precision=lax.Precision.HIGHEST,
                                  preferred_element_type=jnp.float32).reshape(aw.shape)
        for l in range(layers):
            wm[g, l], wv[g, l] = outer_update(wm[g, l], wv[g, l], aw[l, pl.ds(0, n)])
        for q in range(quads):
            lanes = pl.ds(q * LANES, LANES)
            four = swap_blocks([wm[g, l, :, lanes] for l in range(layers)], masks)
            for j, value in enumerate(four):
                back[k, pl.ds((4 * q + j) * n, n)] = value
        spread_start(back, gw.at[g], me * rows[k], k, bw_send, bw_recv)
        for copy in state_stores[2 + 2 * g:4 + 2 * g]:
            copy.start()

    state_stores = [pltpu.make_async_copy(qm, qm_out, out_sem.at[0]), pltpu.make_async_copy(qv, qv_out, out_sem.at[1])]
    for g in range(2):
        state_stores += [pltpu.make_async_copy(wm.at[g], wm_out.at[g], out_sem.at[2 + g]),
                         pltpu.make_async_copy(wv.at[g], wv_out.at[g], out_sem.at[4 + g])]
    wt_stores = [pltpu.make_async_copy(yw.at[g], wt_out.at[g], out_sem.at[6 + g]) for g in range(2)]
    qt_stores = [pltpu.make_async_copy(yq.at[j], qt_out.at[j], out_sem.at[8 + j])
                 for j in range(reps)]

    def gather_copies(k):
        def same(slot, part, i, target):
            there = gathered(k, slot, part)
            return remote(there, there, (ag_send, ag_recv), k, i, target)

        return (same(me, 0, 0, after), same(me, 1, 1, before),
                same(me, 1, 2, after), same(me, 0, 3, before),
                same(before, 0, 4, after), same(after, 1, 5, before))

    gather = [gather_copies(k) for k in chunks]

    def gather_start(k):
        if k:
            spread_arrived(gw.at[k - 1, pl.ds(pl.multiple_of(me * rows[k], 8), rows[k])], k, bw_recv)
        else:
            spread_arrived(gq, 0, bw_recv)
            for g in range(groups):
                tile = gq[pl.ds(g, block, stride=groups)].T
                yq[me, :, g] = tile.reshape(layers, width, block)
        for copy in gather[k][:4]:
            copy.start()

    def gather_relay(k):
        for i in range(2):
            gather[k][i].wait_recv()
            gather[k][4 + i].start()

    def gather_finish(k):
        for copy in gather[k][2:]:
            copy.wait_recv()
        if k:
            from_rows(k - 1)
            wt_stores[k - 1].start()
        else:
            for copy in qt_stores:
                copy.start()

    def wait_all(copies):
        for copy in copies:
            copy.wait()

    wait_all(loads)
    scatter_start(0)
    to_rows(0)
    scatter_start(1)
    scatter_relay(0)
    hear_line()
    to_rows(1)
    scatter_start(2)
    hear_ring()
    scatter_relay(1)
    hear_partner()
    scatter_finish(0)
    scatter_relay(2)
    scatter_finish(1)
    wait_all(state_loads)
    own_qkv()
    scatter_finish(2)
    own_wi(0)
    gather_start(0)
    own_wi(1)
    gather_relay(0)
    gather_start(1)
    gather_relay(1)
    gather_finish(0)
    gather_start(2)
    gather_relay(2)
    gather_finish(1)
    gather_finish(2)
    for k in chunks:
        for copy in scatter[k] + gather[k]:
            copy.wait_send()
        spread_sent(send, k, fw_send)
        spread_sent(back, k, bw_send)
    wait_all(state_stores + wt_stores + qt_stores)


def write_out(qm, qv, wm, wv, yq, yw, qm_out, qv_out, wm_out, wv_out, qt_out, wt_out, sem):
    reps, block = yq.shape[0], yq.shape[4]
    copies = [(qm, qm_out), (qv, qv_out)]
    for g in range(2):
        copies += [(wm.at[g], wm_out.at[:, :, g, :]), (wv.at[g], wv_out.at[:, :, g, :]),
                   (yw.at[g], wt_out.at[:, :, g, :])]
    copies += [(yq.at[j], qt_out.at[:, :, :, pl.ds(j * block, block)]) for j in range(reps)]
    copies = [pltpu.make_async_copy(src, dst, sem.at[i]) for i, (src, dst) in enumerate(copies)]
    for copy in copies:
        copy.start()
    for copy in copies:
        copy.wait()


def per_device(qkv_delta, wi_delta, basis, qkv_master, qkv_momentum, wi_master, wi_momentum):
    reps, shards = lax.axis_size("rep"), lax.axis_size("shard")
    _, layers, width, groups, cols = qkv_delta.shape
    ff = wi_delta.shape[4]
    share_q, total = qkv_master.shape[3:]
    share_w = wi_master.shape[3]
    block = cols // reps
    tall = max(groups * share_q, share_w) * shards
    f32 = jnp.float32
    shape = functools.partial(jax.ShapeDtypeStruct, dtype=f32)
    vmem = lambda *dims: pltpu.VMEM(dims, f32)
    dma = pltpu.SemaphoreType.DMA
    anywhere = pl.BlockSpec(memory_space=pl.ANY)
    padded = -(-share_w // 8) * 8
    outs = pl.pallas_call(
        functools.partial(kernel, reps, shards),
        out_shape=(
            shape((layers, groups, share_q, total)), shape((layers, groups, share_q, total)),
            shape((2, layers, share_w, total)), shape((2, layers, share_w, total)),
            shape((reps, layers, groups, width, block)), shape((2, layers, width, ff)),
        ),
        in_specs=[pl.BlockSpec(memory_space=pltpu.HBM)] * 7,
        out_specs=(anywhere,) * 6,
        scratch_shapes=[
            vmem(reps, layers, groups, width, block),
            vmem(2, layers, width, ff),
            vmem(2, ff, LANES),
            *[vmem(2, layers // 2, groups, width, block)] * 4,
            *[vmem(2, 2, ff // reps // 2, LANES)] * 4,
            vmem(3, tall, LANES), vmem(3, tall, LANES), vmem(3, tall, LANES),
            vmem(groups * share_q * shards, LANES),
            vmem(reps, layers, groups, width, block),
            vmem(2, ff, LANES),
            vmem(2, layers, width, ff),
            vmem(layers, groups, share_q, total),
            vmem(layers, padded, total), vmem(layers, padded, total),
            vmem(basis.shape[1], total),
            vmem(layers, groups, share_q, total), vmem(layers, groups, share_q, total),
            vmem(2, layers, share_w, total), vmem(2, layers, share_w, total),
            dma((3, 6)), dma((3, 6)), dma((3, 6)), dma((3, 6)),
            dma((3,)), dma((3,)), dma((3,)), dma((3,)),
            dma((10 + reps,)), dma((8 + reps,)), pltpu.SemaphoreType.REGULAR((6,)),
        ],
        compiler_params=pltpu.CompilerParams(
            collective_id=0, has_side_effects=True, vmem_limit_bytes=48 * 2**20
        ),
    )(*(pltpu.with_memory_space_constraint(x, pltpu.HBM) for x in (
        jnp.transpose(qkv_delta[0], (0, 2, 1, 3)), wi_delta[0], basis.T, qkv_master[0], qkv_momentum[0],
        jnp.transpose(wi_master[0], (0, 2, 1, 3)), jnp.transpose(wi_momentum[0], (0, 2, 1, 3)),
    )))
    qm, qv, wm, wv, qt, wt = pl.pallas_call(
        write_out,
        out_shape=(
            shape((layers, groups, share_q, total)), shape((layers, groups, share_q, total)),
            shape((layers, share_w, 2, total)), shape((layers, share_w, 2, total)),
            shape((layers, groups, width, cols)), shape((layers, width, 2, ff)),
        ),
        in_specs=[anywhere] * 6,
        out_specs=(anywhere,) * 6,
        scratch_shapes=[dma((8 + reps,))],
        compiler_params=pltpu.CompilerParams(vmem_limit_bytes=2**17),
    )(*outs)
    return (qm[None], qv[None], jnp.transpose(wm, (0, 2, 1, 3))[None], jnp.transpose(wv, (0, 2, 1, 3))[None],
            jnp.transpose(qt, (0, 2, 1, 3)), wt)


def solution(mesh):
    delta = P("rep", None, "shard", None, "tp")
    state = P("tp", None, None, ("rep", "shard"), None)
    train = P(None, "shard", None, "tp")
    return jax.shard_map(
        per_device, mesh=mesh, in_specs=(delta, delta, P(), state, state, state, state),
        out_specs=(state, state, state, state, train, train), check_vma=False,
    )
```

```python
import functools

import jax
import jax.numpy as jnp
from jax import lax
from jax.experimental import pallas as pl
from jax.experimental.pallas import tpu as pltpu
from jax.sharding import PartitionSpec as P

LANES = 128


def swap_blocks(four, masks):
    low_half, even = masks
    a, b, c, d = four
    a, c = jnp.where(low_half, a, pltpu.roll(c, 64, 1)), jnp.where(low_half, pltpu.roll(a, 64, 1), c)
    b, d = jnp.where(low_half, b, pltpu.roll(d, 64, 1)), jnp.where(low_half, pltpu.roll(b, 64, 1), d)
    a, b = jnp.where(even, a, pltpu.roll(b, 32, 1)), jnp.where(even, pltpu.roll(a, 96, 1), b)
    c, d = jnp.where(even, c, pltpu.roll(d, 32, 1)), jnp.where(even, pltpu.roll(c, 96, 1), d)
    return a, b, c, d


def block_masks(rows):
    lane = lax.broadcasted_iota(jnp.int32, (rows, LANES), 1)
    return lane < 64, lax.rem(lax.div(lane, 32), 2) == 0


def chunk_rows(chunk, share_q, share_w):
    return share_q if chunk[0] == "q" else share_w


def outer_update(master, momentum, average):
    momentum_new = 0.9 * momentum + average
    return master - 0.7 * (average + 0.9 * momentum_new), momentum_new


MOMENTUM = 0.7 * 0.9 * 0.9
AVERAGE = 0.7 * 1.9
CHUNKS = (("w", 0), ("w", 1), ("q", 0))


def kernel(reps, shards, chunks, *refs):
    refs = list(refs)

    def take(n):
        taken = refs[:n]
        del refs[:n]
        return taken

    qkv_in, wi_in, basis_in, qm_in, qv_in, wm_in, wv_in = take(7)
    qm_out, qv_out, wm_out, wv_out, qt_out, wt_out = take(6)
    far, direct, joined, partial, send, got, back, held, formed = (take(len(chunks)) for _ in range(9))
    xq, xw, yq, yw, dq, dw, aw, basis, qm, qv, wm, wv = take(12)
    rs_send, rs_recv, ag_send, ag_recv, fw_send, fw_recv, bw_send, bw_recv, in_sem, out_sem, news = refs
    layers, groups, width, block = xq.shape[1:]
    share_q, share_w = qm.shape[2], wm.shape[2]
    me = lax.axis_index("rep")
    own = lax.axis_index("shard")
    after = lax.rem(me + 1, reps)
    before = lax.rem(me + reps - 1, reps)
    across = lax.rem(me + 2, reps)
    quads = shards // 4
    share = tuple(chunk_rows(chunk, groups * share_q, share_w) for chunk in chunks)
    rows = tuple(shards * n for n in share)
    half = tuple(n // 2 for n in rows)

    loads = [pltpu.make_async_copy(qkv_in.at[:, :, :, pl.ds(j * block, block)], xq.at[j], in_sem.at[10 + j])
             for j in range(reps)]
    wi_loads = [pltpu.make_async_copy(wi_in.at[:, :, g, :], xw.at[g], in_sem.at[1 + g]) for g in range(2)]
    state_loads = [pltpu.make_async_copy(qm_in, qm, in_sem.at[3]), pltpu.make_async_copy(qv_in, qv, in_sem.at[4]),
                   pltpu.make_async_copy(basis_in, basis, in_sem.at[5])]
    for g in range(2):
        state_loads += [pltpu.make_async_copy(wm_in.at[:, :, g, :], wm.at[g], in_sem.at[6 + g]),
                        pltpu.make_async_copy(wv_in.at[:, :, g, :], wv.at[g], in_sem.at[8 + g])]
    for copy in loads + wi_loads + state_loads:
        copy.start()

    cores, line = 2, min(4, shards // 2)
    ring = shards // (cores * line)
    core = lax.rem(own, cores)
    spot = lax.rem(lax.div(own, cores), line)
    partner = own + 1 - 2 * core
    up, down = own + cores, own - cores
    has_up, has_down = spot < line - 1, spot > 0
    stride = cores * line
    forth = lax.rem(own + stride, shards)
    aback = lax.rem(own + shards - stride, shards)

    def tell(sem, **target):
        pl.semaphore_signal(sem, inc=1, device_id=target)

    barrier = pltpu.get_barrier_semaphore()
    tell(barrier, rep=after)
    tell(barrier, rep=before)
    tell(barrier, shard=partner)
    if ring > 1:
        tell(barrier, shard=forth)
        tell(barrier, shard=aback)
    pl.when(has_up)(lambda: tell(barrier, shard=up))
    pl.when(has_down)(lambda: tell(barrier, shard=down))
    dw[...] = jnp.zeros_like(dw)
    near = 3 + (2 if ring > 1 else 0)
    pl.semaphore_wait(barrier, near + has_up.astype(jnp.int32) + has_down.astype(jnp.int32))

    def pass_on(slot, here, **target):
        pl.when(here)(lambda: tell(news.at[slot], **target))

    def hear(slot, here):
        @pl.when(here)
        def _():
            pl.semaphore_wait(news.at[slot], 1)

    second, third = spot >= 2, spot >= 3
    second_last, third_last = spot <= line - 3, spot <= line - 4

    def round_1():
        pass_on(0, jnp.logical_and(has_up, has_down), shard=up)
        pass_on(1, jnp.logical_and(has_up, has_down), shard=down)
        if ring > 1:
            tell(news.at[2], shard=forth)

    def round_2():
        hear(0, second)
        hear(1, second_last)
        pass_on(3, jnp.logical_and(has_up, second), shard=up)
        pass_on(4, jnp.logical_and(has_down, second_last), shard=down)
        if ring > 1:
            pl.semaphore_wait(news.at[2], 1)

    def round_3():
        hear(3, third)
        hear(4, third_last)
        for i in range(1, ring):
            tell(news.at[5], shard=lax.rem(own + i * stride, shards))

    def round_4():
        if ring > 1:
            pl.semaphore_wait(news.at[5], ring - 1)
        tell(news.at[6], shard=partner)

    def round_5():
        pl.semaphore_wait(news.at[6], 1)

    def half_of(k, slot, part, q_ref, w_refs):
        if chunks[k][0] == "q":
            return q_ref.at[slot, pl.ds(part * (layers // 2), layers // 2)]
        return w_refs[k].at[pl.ds(pl.multiple_of(slot * rows[k] + part * half[k], 8), half[k])]

    def term(k, slot, part):
        return half_of(k, slot, part, xq, formed)

    def gathered(k, slot, part):
        return half_of(k, slot, part, yq, held)

    def remote(src, dst, sems, k, i, target):
        return pltpu.make_async_remote_copy(
            src_ref=src, dst_ref=dst, send_sem=sems[0].at[k, i], recv_sem=sems[1].at[k, i],
            device_id={"rep": target}, device_id_type=pl.DeviceIdType.MESH)

    def scatter_copies(k):
        sems = (rs_send, rs_recv)
        return (
            remote(term(k, across, 0), far[k].at[0], sems, k, 0, after),
            remote(term(k, across, 1), far[k].at[1], sems, k, 1, before),
            remote(term(k, after, 1), direct[k].at[1], sems, k, 2, after),
            remote(term(k, before, 0), direct[k].at[0], sems, k, 3, before),
            remote(partial[k].at[0], joined[k].at[0], sems, k, 4, after),
            remote(partial[k].at[1], joined[k].at[1], sems, k, 5, before),
        )

    scatter = [scatter_copies(k) for k in range(len(chunks))]

    def scatter_start(k):
        for copy in scatter[k][:4]:
            copy.start()

    def scatter_relay(k):
        for i, target in enumerate((after, before)):
            scatter[k][i].wait_recv()
            partial[k][i] = far[k][i] + term(k, target, i)[...]
            scatter[k][4 + i].start()

    def scatter_finish(k):
        for copy in scatter[k][2:]:
            copy.wait_recv()
        sums = [term(k, me, i)[...] + direct[k][i] + joined[k][i] for i in range(2)]
        if chunks[k][0] == "w":
            send[k][pl.ds(0, half[k])] = sums[0]
            send[k][pl.ds(half[k], half[k])] = sums[1]
        else:
            full = jnp.concatenate(sums, 0)
            spread_arrived(held[k], k, bw_recv)
            for g in range(groups):
                early = held[k][every(g, block, groups)].T.reshape(layers, width, block)
                yq[me, :, g] = early - AVERAGE / reps * full[:, g]
            for copy in gather[k][:4]:
                copy.start()
            for g in range(groups):
                send[k][every(g, block, groups)] = full[:, g].reshape(layers * width, block).T
        spread_start(send[k], got[k], 0, k, fw_send, fw_recv)

    def spread_start(src, dst, base, k, sem, other):
        n = share[k]

        def one(j, carry):
            target = lax.rem(own + j, shards)
            pltpu.make_async_remote_copy(
                src_ref=src.at[pl.ds(target * n, n)], dst_ref=dst.at[pl.ds(base + own * n, n)],
                send_sem=sem.at[k], recv_sem=other.at[k],
                device_id={"shard": target}, device_id_type=pl.DeviceIdType.MESH).start()
            return carry

        lax.fori_loop(1, shards, one, 0)
        pltpu.make_async_copy(src.at[pl.ds(own * n, n)], dst.at[pl.ds(base + own * n, n)], other.at[k]).start()

    def spread_sent(src, k, sem):
        part = src.at[pl.ds(0, (shards - 1) * share[k])]
        pltpu.make_async_copy(part, part, sem.at[k]).wait()

    def spread_arrived(dst, k, sem):
        pltpu.make_async_copy(dst, dst, sem.at[k]).wait()

    def every(start, count, step):
        return pl.ds(start, count, stride=step) if step > 1 else pl.ds(start, count)

    def to_rows(k):
        g = chunks[k][1]
        wi_loads[g].wait()
        for j in range(xw.shape[3] // LANES):
            tile = xw[g, :, :, pl.ds(j * LANES, LANES)].reshape(layers * width, LANES)
            formed[k][pl.ds(j * LANES, LANES)] = tile.T

    def from_rows(k):
        for j in range(yw.shape[3] // LANES):
            tile = held[k][pl.ds(j * LANES, LANES)].T
            yw[chunks[k][1], :, :, pl.ds(j * LANES, LANES)] = tile.reshape(layers, width, LANES)

    def own_rows(k):
        (own_qkv if chunks[k][0] == "q" else own_wi)(k)

    def early_qkv(k):
        masks = block_masks(share_q)
        for l in range(layers):
            dq[l] = qm[l] - MOMENTUM * qv[l]
        for q in range(quads):
            lanes = pl.ds(q * LANES, LANES)
            for g in range(groups):
                four = swap_blocks([dq[l, g, :, lanes] for l in range(layers)], masks)
                for j, value in enumerate(four):
                    back[k][every((4 * q + j) * share[k] + g, share_q, groups)] = value
        spread_start(back[k], held[k], 0, k, bw_send, bw_recv)

    def own_qkv(k):
        spread_arrived(got[k], k, fw_recv)
        masks = block_masks(share_q)
        for q in range(quads):
            lanes = pl.ds(q * LANES, LANES)
            for g in range(groups):
                four = [got[k][every((4 * q + j) * share[k] + g, share_q, groups)] for j in range(4)]
                for l, value in enumerate(swap_blocks(four, masks)):
                    dq[l, g, :, lanes] = value
        for l in range(layers):
            qm[l], qv[l] = outer_update(qm[l], qv[l], dq[l] / reps)
        for copy in state_stores[:2]:
            copy.start()

    def own_wi(k):
        g, n = chunks[k][1], share_w
        spread_arrived(got[k], k, fw_recv)
        masks = block_masks(n)
        for q in range(quads):
            lanes = pl.ds(q * LANES, LANES)
            four = [got[k][pl.ds((4 * q + j) * n, n)] for j in range(4)]
            for l, value in enumerate(swap_blocks(four, masks)):
                dw[l, pl.ds(0, n), lanes] = value
        total = dw[...].reshape(-1, dw.shape[2])
        coef = lax.dot_general(total, basis[...], (((1,), (1,)), ((), ())), precision=lax.Precision.HIGHEST,
                               preferred_element_type=jnp.float32) / reps
        aw[...] = lax.dot_general(
            coef, basis[...], (((1,), (0,)), ((), ())), precision=lax.Precision.HIGHEST,
            preferred_element_type=jnp.float32).reshape(aw.shape)
        for l in range(layers):
            wm[g, l], wv[g, l] = outer_update(wm[g, l], wv[g, l], aw[l, pl.ds(0, n)])
        for q in range(quads):
            lanes = pl.ds(q * LANES, LANES)
            four = swap_blocks([wm[g, l, :, lanes] for l in range(layers)], masks)
            for j, value in enumerate(four):
                back[k][pl.ds((4 * q + j) * n, n)] = value
        spread_start(back[k], held[k], me * rows[k], k, bw_send, bw_recv)
        for copy in state_stores[2 + 2 * g:4 + 2 * g]:
            copy.start()

    state_stores = [pltpu.make_async_copy(qm, qm_out, out_sem.at[0]), pltpu.make_async_copy(qv, qv_out, out_sem.at[1])]
    for g in range(2):
        state_stores += [pltpu.make_async_copy(wm.at[g], wm_out.at[g], out_sem.at[2 + g]),
                         pltpu.make_async_copy(wv.at[g], wv_out.at[g], out_sem.at[4 + g])]
    wt_stores = [pltpu.make_async_copy(yw.at[g], wt_out.at[g], out_sem.at[6 + g]) for g in range(2)]
    qt_stores = [pltpu.make_async_copy(yq.at[j], qt_out.at[j], out_sem.at[8 + j])
                 for j in range(reps)]

    def gather_copies(k):
        def same(slot, part, i, target):
            there = gathered(k, slot, part)
            return remote(there, there, (ag_send, ag_recv), k, i, target)

        return (same(me, 0, 0, after), same(me, 1, 1, before),
                same(me, 1, 2, after), same(me, 0, 3, before),
                same(before, 0, 4, after), same(after, 1, 5, before))

    gather = [gather_copies(k) for k in range(len(chunks))]

    def gather_start(k):
        spread_arrived(held[k].at[pl.ds(pl.multiple_of(me * rows[k], 8), rows[k])], k, bw_recv)
        for copy in gather[k][:4]:
            copy.start()

    def gather_relay(k):
        for i in range(2):
            gather[k][i].wait_recv()
            gather[k][4 + i].start()

    def gather_finish(k):
        for copy in gather[k][2:]:
            copy.wait_recv()
        if chunks[k][0] == "w":
            from_rows(k)
            wt_stores[chunks[k][1]].start()
        else:
            for copy in qt_stores:
                copy.start()

    def wait_all(copies):
        for copy in copies:
            copy.wait()

    wait_all(loads)
    to_rows(0)
    scatter_start(0)
    round_1()
    to_rows(1)
    round_2()
    scatter_relay(0)
    scatter_start(1)
    round_3()
    round_4()
    round_5()
    wait_all(state_loads)
    early_qkv(2)
    scatter_finish(0)
    scatter_relay(1)
    scatter_start(2)
    scatter_finish(1)
    scatter_relay(2)
    own_rows(0)
    scatter_finish(2)
    own_rows(1)
    gather_relay(2)
    gather_start(0)
    own_rows(2)
    gather_relay(0)
    gather_start(1)
    gather_finish(2)
    gather_finish(0)
    gather_relay(1)
    gather_finish(1)
    for k in range(len(chunks)):
        for copy in scatter[k] + gather[k]:
            copy.wait_send()
        spread_sent(send[k], k, fw_send)
        spread_sent(back[k], k, bw_send)
    wait_all(state_stores + wt_stores + qt_stores)


def write_out(qm, qv, wm, wv, yq, yw, qm_out, qv_out, wm_out, wv_out, qt_out, wt_out, sem):
    reps, block = yq.shape[0], yq.shape[4]
    copies = [(qm, qm_out), (qv, qv_out)]
    for g in range(2):
        copies += [(wm.at[g], wm_out.at[:, :, g, :]), (wv.at[g], wv_out.at[:, :, g, :]),
                   (yw.at[g], wt_out.at[:, :, g, :])]
    copies += [(yq.at[j], qt_out.at[:, :, :, pl.ds(j * block, block)]) for j in range(reps)]
    copies = [pltpu.make_async_copy(src, dst, sem.at[i]) for i, (src, dst) in enumerate(copies)]
    for copy in copies:
        copy.start()
    for copy in copies:
        copy.wait()


def per_device(qkv_delta, wi_delta, basis, qkv_master, qkv_momentum, wi_master, wi_momentum):
    reps, shards = lax.axis_size("rep"), lax.axis_size("shard")
    _, layers, width, groups, cols = qkv_delta.shape
    ff = wi_delta.shape[4]
    share_q, total = qkv_master.shape[3:]
    share_w = wi_master.shape[3]
    block = cols // reps
    chunks = CHUNKS
    sizes = [chunk_rows(chunk, groups * share_q, share_w) * shards for chunk in chunks]
    wide = [chunk[0] == "w" for chunk in chunks]
    f32 = jnp.float32
    shape = functools.partial(jax.ShapeDtypeStruct, dtype=f32)
    vmem = lambda *dims: pltpu.VMEM(dims, f32)
    dma = pltpu.SemaphoreType.DMA
    anywhere = pl.BlockSpec(memory_space=pl.ANY)
    padded = -(-share_w // 8) * 8
    outs = pl.pallas_call(
        functools.partial(kernel, reps, shards, chunks),
        out_shape=(
            shape((layers, groups, share_q, total)), shape((layers, groups, share_q, total)),
            shape((2, layers, share_w, total)), shape((2, layers, share_w, total)),
            shape((reps, layers, groups, width, block)), shape((2, layers, width, ff)),
        ),
        in_specs=[pl.BlockSpec(memory_space=pltpu.HBM)] * 7,
        out_specs=(anywhere,) * 6,
        scratch_shapes=[
            *[vmem(2, n // 2, LANES) if wi else vmem(2, layers // 2, groups, width, block)
              for n, wi in zip(sizes, wide)] * 4,
            *[vmem(n, LANES) for n in sizes] * 3,
            *[vmem(reps * n if wi else n, LANES) for n, wi in zip(sizes, wide)],
            *[vmem(reps * n if wi else 8, LANES) for n, wi in zip(sizes, wide)],
            vmem(reps, layers, groups, width, block), vmem(2, layers, width, ff),
            vmem(reps, layers, groups, width, block), vmem(2, layers, width, ff),
            vmem(layers, groups, share_q, total),
            vmem(layers, padded, total), vmem(layers, padded, total),
            vmem(basis.shape[1], total),
            vmem(layers, groups, share_q, total), vmem(layers, groups, share_q, total),
            vmem(2, layers, share_w, total), vmem(2, layers, share_w, total),
            *[dma((len(chunks), 6))] * 4, *[dma((len(chunks),))] * 4,
            dma((10 + reps,)), dma((8 + reps,)), pltpu.SemaphoreType.REGULAR((7,)),
        ],
        compiler_params=pltpu.CompilerParams(
            collective_id=0, has_side_effects=True, vmem_limit_bytes=48 * 2**20
        ),
    )(*(pltpu.with_memory_space_constraint(x, pltpu.HBM) for x in (
        jnp.transpose(qkv_delta[0], (0, 2, 1, 3)), wi_delta[0], basis.T, qkv_master[0], qkv_momentum[0],
        jnp.transpose(wi_master[0], (0, 2, 1, 3)), jnp.transpose(wi_momentum[0], (0, 2, 1, 3)),
    )))
    qm, qv, wm, wv, qt, wt = pl.pallas_call(
        write_out,
        out_shape=(
            shape((layers, groups, share_q, total)), shape((layers, groups, share_q, total)),
            shape((layers, share_w, 2, total)), shape((layers, share_w, 2, total)),
            shape((layers, groups, width, cols)), shape((layers, width, 2, ff)),
        ),
        in_specs=[anywhere] * 6,
        out_specs=(anywhere,) * 6,
        scratch_shapes=[dma((8 + reps,))],
        compiler_params=pltpu.CompilerParams(vmem_limit_bytes=2**17),
    )(*outs)
    return (qm[None], qv[None], jnp.transpose(wm, (0, 2, 1, 3))[None], jnp.transpose(wv, (0, 2, 1, 3))[None],
            jnp.transpose(qt, (0, 2, 1, 3)), wt)


def solution(mesh):
    delta = P("rep", None, "shard", None, "tp")
    state = P("tp", None, None, ("rep", "shard"), None)
    train = P(None, "shard", None, "tp")
    return jax.shard_map(
        per_device, mesh=mesh, in_specs=(delta, delta, P(), state, state, state, state),
        out_specs=(state, state, state, state, train, train), check_vma=False,
    )
```

```python
import functools

import jax
import jax.numpy as jnp
from jax import lax
from jax.experimental import pallas as pl
from jax.experimental.pallas import tpu as pltpu
from jax.sharding import PartitionSpec as P

LANES = 128


def swap_blocks(four, masks):
    low_half, even = masks
    a, b, c, d = four
    a, c = jnp.where(low_half, a, pltpu.roll(c, 64, 1)), jnp.where(low_half, pltpu.roll(a, 64, 1), c)
    b, d = jnp.where(low_half, b, pltpu.roll(d, 64, 1)), jnp.where(low_half, pltpu.roll(b, 64, 1), d)
    a, b = jnp.where(even, a, pltpu.roll(b, 32, 1)), jnp.where(even, pltpu.roll(a, 96, 1), b)
    c, d = jnp.where(even, c, pltpu.roll(d, 32, 1)), jnp.where(even, pltpu.roll(c, 96, 1), d)
    return a, b, c, d


def block_masks(rows):
    lane = lax.broadcasted_iota(jnp.int32, (rows, LANES), 1)
    return lane < 64, lax.rem(lax.div(lane, 32), 2) == 0


def chunk_rows(chunk, share_q, share_w):
    return share_q if chunk[0] == "q" else share_w


def outer_update(master, momentum, average):
    momentum_new = 0.9 * momentum + average
    return master - 0.7 * (average + 0.9 * momentum_new), momentum_new


MOMENTUM = 0.7 * 0.9 * 0.9
AVERAGE = 0.7 * 1.9
CHUNKS = (("w", 0), ("w", 1), ("q", 0))


def kernel(reps, shards, chunks, *refs):
    refs = list(refs)

    def take(n):
        taken = refs[:n]
        del refs[:n]
        return taken

    qkv_in, wi_in, basis_in, qm_in, qv_in, wm_in, wv_in = take(7)
    qm_out, qv_out, wm_out, wv_out, qt_out, wt_out = take(6)
    far, direct, joined, partial, send, got, back, held, formed = (take(len(chunks)) for _ in range(9))
    xq, xw, yq, yw, dq, dw, aw, basis, qm, qv, wm, wv = take(12)
    rs_send, rs_recv, ag_send, ag_recv, fw_send, fw_recv, bw_send, bw_recv, in_sem, out_sem, news = refs
    layers, groups, width, block = xq.shape[1:]
    share_q, share_w = qm.shape[2], wm.shape[2]
    me = lax.axis_index("rep")
    own = lax.axis_index("shard")
    after = lax.rem(me + 1, reps)
    before = lax.rem(me + reps - 1, reps)
    across = lax.rem(me + 2, reps)
    quads = shards // 4
    share = tuple(chunk_rows(chunk, groups * share_q, share_w) for chunk in chunks)
    rows = tuple(shards * n for n in share)
    half = tuple(n // 2 for n in rows)

    cores, line = 2, min(4, shards // 2)
    ring = shards // (cores * line)
    core = lax.rem(own, cores)
    spot = lax.rem(lax.div(own, cores), line)
    partner = own + 1 - 2 * core
    up, down = own + cores, own - cores
    has_up, has_down = spot < line - 1, spot > 0
    stride = cores * line
    forth = lax.rem(own + stride, shards)
    aback = lax.rem(own + shards - stride, shards)

    def tell(sem, **target):
        pl.semaphore_signal(sem, inc=1, device_id=target)

    barrier = pltpu.get_barrier_semaphore()
    tell(barrier, rep=after)
    tell(barrier, rep=before)
    tell(barrier, shard=partner)
    if ring > 1:
        tell(barrier, shard=forth)
        tell(barrier, shard=aback)
    pl.when(has_up)(lambda: tell(barrier, shard=up))
    pl.when(has_down)(lambda: tell(barrier, shard=down))
    loads = [pltpu.make_async_copy(qkv_in.at[:, :, :, pl.ds(j * block, block)], xq.at[j], in_sem.at[10 + j])
             for j in range(reps)]
    wi_loads = [pltpu.make_async_copy(wi_in.at[:, :, g, :], xw.at[g], in_sem.at[1 + g]) for g in range(2)]
    state_loads = [pltpu.make_async_copy(qm_in, qm, in_sem.at[3]), pltpu.make_async_copy(qv_in, qv, in_sem.at[4]),
                   pltpu.make_async_copy(basis_in, basis, in_sem.at[5])]
    for g in range(2):
        state_loads += [pltpu.make_async_copy(wm_in.at[:, :, g, :], wm.at[g], in_sem.at[6 + g]),
                        pltpu.make_async_copy(wv_in.at[:, :, g, :], wv.at[g], in_sem.at[8 + g])]
    for copy in wi_loads + loads + state_loads:
        copy.start()

    dw[...] = jnp.zeros_like(dw)
    def enter():
        near = 3 + (2 if ring > 1 else 0)
        pl.semaphore_wait(barrier, near + has_up.astype(jnp.int32) + has_down.astype(jnp.int32))

    def pass_on(slot, here, **target):
        pl.when(here)(lambda: tell(news.at[slot], **target))

    def hear(slot, here):
        @pl.when(here)
        def _():
            pl.semaphore_wait(news.at[slot], 1)

    second, third = spot >= 2, spot >= 3
    second_last, third_last = spot <= line - 3, spot <= line - 4

    def round_1():
        pass_on(0, jnp.logical_and(has_up, has_down), shard=up)
        pass_on(1, jnp.logical_and(has_up, has_down), shard=down)
        if ring > 1:
            tell(news.at[2], shard=forth)

    def round_2():
        hear(0, second)
        hear(1, second_last)
        pass_on(3, jnp.logical_and(has_up, second), shard=up)
        pass_on(4, jnp.logical_and(has_down, second_last), shard=down)
        if ring > 1:
            pl.semaphore_wait(news.at[2], 1)

    def round_3():
        hear(3, third)
        hear(4, third_last)
        for i in range(1, ring):
            tell(news.at[5], shard=lax.rem(own + i * stride, shards))

    def round_4():
        if ring > 1:
            pl.semaphore_wait(news.at[5], ring - 1)
        tell(news.at[6], shard=partner)

    def round_5():
        pl.semaphore_wait(news.at[6], 1)

    def half_of(k, slot, part, q_ref, w_refs):
        if chunks[k][0] == "q":
            return q_ref.at[slot, pl.ds(part * (layers // 2), layers // 2)]
        return w_refs[k].at[pl.ds(pl.multiple_of(slot * rows[k] + part * half[k], 8), half[k])]

    def term(k, slot, part):
        return half_of(k, slot, part, xq, formed)

    def gathered(k, slot, part):
        return half_of(k, slot, part, yq, held)

    def remote(src, dst, sems, k, i, target):
        return pltpu.make_async_remote_copy(
            src_ref=src, dst_ref=dst, send_sem=sems[0].at[k, i], recv_sem=sems[1].at[k, i],
            device_id={"rep": target}, device_id_type=pl.DeviceIdType.MESH)

    def scatter_copies(k):
        sems = (rs_send, rs_recv)
        return (
            remote(term(k, across, 0), far[k].at[0], sems, k, 0, after),
            remote(term(k, across, 1), far[k].at[1], sems, k, 1, before),
            remote(term(k, after, 1), direct[k].at[1], sems, k, 2, after),
            remote(term(k, before, 0), direct[k].at[0], sems, k, 3, before),
            remote(partial[k].at[0], joined[k].at[0], sems, k, 4, after),
            remote(partial[k].at[1], joined[k].at[1], sems, k, 5, before),
        )

    scatter = [scatter_copies(k) for k in range(len(chunks))]

    def scatter_start(k):
        for copy in scatter[k][:4]:
            copy.start()

    def scatter_relay(k):
        for i, target in enumerate((after, before)):
            scatter[k][i].wait_recv()
            partial[k][i] = far[k][i] + term(k, target, i)[...]
            scatter[k][4 + i].start()

    def summed(k):
        return [term(k, me, i)[...] + direct[k][i] + joined[k][i] for i in range(2)]

    def scatter_finish(k):
        for copy in scatter[k][2:]:
            copy.wait_recv()
        sums = summed(k)
        if chunks[k][0] == "w":
            send[k][pl.ds(0, half[k])] = sums[0]
            send[k][pl.ds(half[k], half[k])] = sums[1]
            spread_start(send[k], got[k], 0, k, fw_send, fw_recv)
        else:
            full = jnp.concatenate(sums, 0)
            spread_arrived(held[k], k, bw_recv)
            for g in range(groups):
                early = held[k][every(g, block, groups)].T.reshape(layers, width, block)
                yq[me, :, g] = early - AVERAGE / reps * full[:, g]
            for copy in gather[k][:4]:
                copy.start()

    def spread_qkv(k):
        full = jnp.concatenate(summed(k), 0)
        for g in range(groups):
            send[k][every(g, block, groups)] = full[:, g].reshape(layers * width, block).T
        spread_start(send[k], got[k], 0, k, fw_send, fw_recv)

    def spread_start(src, dst, base, k, sem, other):
        n = share[k]

        for step in sorted(range(1, shards), key=lambda step: (-min(step % stride, stride - step % stride), step)):
            target = lax.rem(own + step, shards)
            pltpu.make_async_remote_copy(
                src_ref=src.at[pl.ds(target * n, n)], dst_ref=dst.at[pl.ds(base + own * n, n)],
                send_sem=sem.at[k], recv_sem=other.at[k],
                device_id={"shard": target}, device_id_type=pl.DeviceIdType.MESH).start()
        pltpu.make_async_copy(src.at[pl.ds(own * n, n)], dst.at[pl.ds(base + own * n, n)], other.at[k]).start()

    def spread_sent(src, k, sem):
        part = src.at[pl.ds(0, (shards - 1) * share[k])]
        pltpu.make_async_copy(part, part, sem.at[k]).wait()

    def spread_arrived(dst, k, sem):
        pltpu.make_async_copy(dst, dst, sem.at[k]).wait()

    def every(start, count, step):
        return pl.ds(start, count, stride=step) if step > 1 else pl.ds(start, count)

    def to_rows(k):
        g = chunks[k][1]
        wi_loads[g].wait()
        for j in range(xw.shape[3] // LANES):
            tile = xw[g, :, :, pl.ds(j * LANES, LANES)].reshape(layers * width, LANES)
            formed[k][pl.ds(j * LANES, LANES)] = tile.T

    def from_rows(k):
        for j in range(yw.shape[3] // LANES):
            tile = held[k][pl.ds(j * LANES, LANES)].T
            yw[chunks[k][1], :, :, pl.ds(j * LANES, LANES)] = tile.reshape(layers, width, LANES)

    def own_rows(k):
        (own_qkv if chunks[k][0] == "q" else own_wi)(k)

    def early_qkv(k):
        masks = block_masks(share_q)
        for l in range(layers):
            dq[l] = qm[l] - MOMENTUM * qv[l]
        for q in range(quads):
            lanes = pl.ds(q * LANES, LANES)
            for g in range(groups):
                four = swap_blocks([dq[l, g, :, lanes] for l in range(layers)], masks)
                for j, value in enumerate(four):
                    back[k][every((4 * q + j) * share[k] + g, share_q, groups)] = value
        spread_start(back[k], held[k], 0, k, bw_send, bw_recv)

    def own_qkv(k):
        spread_arrived(got[k], k, fw_recv)
        masks = block_masks(share_q)
        for q in range(quads):
            lanes = pl.ds(q * LANES, LANES)
            for g in range(groups):
                four = [got[k][every((4 * q + j) * share[k] + g, share_q, groups)] for j in range(4)]
                for l, value in enumerate(swap_blocks(four, masks)):
                    dq[l, g, :, lanes] = value
        for l in range(layers):
            qm[l], qv[l] = outer_update(qm[l], qv[l], dq[l] / reps)
        for copy in state_stores[:2]:
            copy.start()

    def own_wi(k):
        g, n = chunks[k][1], share_w
        spread_arrived(got[k], k, fw_recv)
        masks = block_masks(n)
        for q in range(quads):
            lanes = pl.ds(q * LANES, LANES)
            four = [got[k][pl.ds((4 * q + j) * n, n)] for j in range(4)]
            for l, value in enumerate(swap_blocks(four, masks)):
                dw[l, pl.ds(0, n), lanes] = value
        total = dw[...].reshape(-1, dw.shape[2])
        coef = lax.dot_general(total, basis[...], (((1,), (1,)), ((), ())), precision=lax.Precision.HIGHEST,
                               preferred_element_type=jnp.float32) / reps
        aw[...] = lax.dot_general(
            coef, basis[...], (((1,), (0,)), ((), ())), precision=lax.Precision.HIGHEST,
            preferred_element_type=jnp.float32).reshape(aw.shape)
        for l in range(layers):
            wm[g, l], wv[g, l] = outer_update(wm[g, l], wv[g, l], aw[l, pl.ds(0, n)])
        for q in range(quads):
            lanes = pl.ds(q * LANES, LANES)
            four = swap_blocks([wm[g, l, :, lanes] for l in range(layers)], masks)
            for j, value in enumerate(four):
                back[k][pl.ds((4 * q + j) * n, n)] = value
        spread_start(back[k], held[k], me * rows[k], k, bw_send, bw_recv)
        for copy in state_stores[2 + 2 * g:4 + 2 * g]:
            copy.start()

    state_stores = [pltpu.make_async_copy(qm, qm_out, out_sem.at[0]), pltpu.make_async_copy(qv, qv_out, out_sem.at[1])]
    for g in range(2):
        state_stores += [pltpu.make_async_copy(wm.at[g], wm_out.at[g], out_sem.at[2 + g]),
                         pltpu.make_async_copy(wv.at[g], wv_out.at[g], out_sem.at[4 + g])]
    wt_stores = [pltpu.make_async_copy(yw.at[g], wt_out.at[g], out_sem.at[6 + g]) for g in range(2)]
    qt_stores = [pltpu.make_async_copy(yq.at[j], qt_out.at[j], out_sem.at[8 + j])
                 for j in range(reps)]

    def gather_copies(k):
        def same(slot, part, i, target):
            there = gathered(k, slot, part)
            return remote(there, there, (ag_send, ag_recv), k, i, target)

        return (same(me, 0, 0, after), same(me, 1, 1, before),
                same(me, 1, 2, after), same(me, 0, 3, before),
                same(before, 0, 4, after), same(after, 1, 5, before))

    gather = [gather_copies(k) for k in range(len(chunks))]

    def gather_start(k):
        spread_arrived(held[k].at[pl.ds(pl.multiple_of(me * rows[k], 8), rows[k])], k, bw_recv)
        for copy in gather[k][:4]:
            copy.start()

    def gather_relay(k):
        for i in range(2):
            gather[k][i].wait_recv()
            gather[k][4 + i].start()

    def gather_finish(k):
        for copy in gather[k][2:]:
            copy.wait_recv()
        if chunks[k][0] == "w":
            from_rows(k)
            wt_stores[chunks[k][1]].start()
        else:
            for copy in qt_stores:
                copy.start()

    def wait_all(copies):
        for copy in copies:
            copy.wait()

    to_rows(0)
    enter()
    scatter_start(0)
    round_1()
    to_rows(1)
    round_2()
    scatter_relay(0)
    scatter_start(1)
    round_3()
    round_4()
    round_5()
    wait_all(state_loads)
    early_qkv(2)
    scatter_finish(0)
    scatter_relay(1)
    wait_all(loads)
    scatter_start(2)
    scatter_finish(1)
    scatter_relay(2)
    own_rows(0)
    scatter_finish(2)
    own_rows(1)
    spread_qkv(2)
    gather_relay(2)
    gather_start(0)
    gather_relay(0)
    gather_start(1)
    gather_finish(0)
    gather_relay(1)
    gather_finish(2)
    own_rows(2)
    gather_finish(1)
    for k in range(len(chunks)):
        for copy in scatter[k] + gather[k]:
            copy.wait_send()
        spread_sent(send[k], k, fw_send)
        spread_sent(back[k], k, bw_send)
    wait_all(state_stores + wt_stores + qt_stores)


def write_out(qm, qv, wm, wv, yq, yw, qm_out, qv_out, wm_out, wv_out, qt_out, wt_out, sem):
    reps, block = yq.shape[0], yq.shape[4]
    copies = [(qm, qm_out), (qv, qv_out)]
    for g in range(2):
        copies += [(wm.at[g], wm_out.at[:, :, g, :]), (wv.at[g], wv_out.at[:, :, g, :]),
                   (yw.at[g], wt_out.at[:, :, g, :])]
    copies += [(yq.at[j], qt_out.at[:, :, :, pl.ds(j * block, block)]) for j in range(reps)]
    copies = [pltpu.make_async_copy(src, dst, sem.at[i]) for i, (src, dst) in enumerate(copies)]
    for copy in copies:
        copy.start()
    for copy in copies:
        copy.wait()


def per_device(qkv_delta, wi_delta, basis, qkv_master, qkv_momentum, wi_master, wi_momentum):
    reps, shards = lax.axis_size("rep"), lax.axis_size("shard")
    _, layers, width, groups, cols = qkv_delta.shape
    ff = wi_delta.shape[4]
    share_q, total = qkv_master.shape[3:]
    share_w = wi_master.shape[3]
    block = cols // reps
    chunks = CHUNKS
    sizes = [chunk_rows(chunk, groups * share_q, share_w) * shards for chunk in chunks]
    wide = [chunk[0] == "w" for chunk in chunks]
    f32 = jnp.float32
    shape = functools.partial(jax.ShapeDtypeStruct, dtype=f32)
    vmem = lambda *dims: pltpu.VMEM(dims, f32)
    dma = pltpu.SemaphoreType.DMA
    anywhere = pl.BlockSpec(memory_space=pl.ANY)
    padded = -(-share_w // 8) * 8
    outs = pl.pallas_call(
        functools.partial(kernel, reps, shards, chunks),
        out_shape=(
            shape((layers, groups, share_q, total)), shape((layers, groups, share_q, total)),
            shape((2, layers, share_w, total)), shape((2, layers, share_w, total)),
            shape((reps, layers, groups, width, block)), shape((2, layers, width, ff)),
        ),
        in_specs=[pl.BlockSpec(memory_space=pltpu.HBM)] * 7,
        out_specs=(anywhere,) * 6,
        scratch_shapes=[
            *[vmem(2, n // 2, LANES) if wi else vmem(2, layers // 2, groups, width, block)
              for n, wi in zip(sizes, wide)] * 4,
            *[vmem(n, LANES) for n in sizes] * 3,
            *[vmem(reps * n if wi else n, LANES) for n, wi in zip(sizes, wide)],
            *[vmem(reps * n if wi else 8, LANES) for n, wi in zip(sizes, wide)],
            vmem(reps, layers, groups, width, block), vmem(2, layers, width, ff),
            vmem(reps, layers, groups, width, block), vmem(2, layers, width, ff),
            vmem(layers, groups, share_q, total),
            vmem(layers, padded, total), vmem(layers, padded, total),
            vmem(basis.shape[1], total),
            vmem(layers, groups, share_q, total), vmem(layers, groups, share_q, total),
            vmem(2, layers, share_w, total), vmem(2, layers, share_w, total),
            *[dma((len(chunks), 6))] * 4, *[dma((len(chunks),))] * 4,
            dma((10 + reps,)), dma((8 + reps,)), pltpu.SemaphoreType.REGULAR((7,)),
        ],
        compiler_params=pltpu.CompilerParams(
            collective_id=0, has_side_effects=True, vmem_limit_bytes=48 * 2**20
        ),
    )(*(pltpu.with_memory_space_constraint(x, pltpu.HBM) for x in (
        jnp.transpose(qkv_delta[0], (0, 2, 1, 3)), wi_delta[0], basis.T, qkv_master[0], qkv_momentum[0],
        jnp.transpose(wi_master[0], (0, 2, 1, 3)), jnp.transpose(wi_momentum[0], (0, 2, 1, 3)),
    )))
    qm, qv, wm, wv, qt, wt = pl.pallas_call(
        write_out,
        out_shape=(
            shape((layers, groups, share_q, total)), shape((layers, groups, share_q, total)),
            shape((layers, share_w, 2, total)), shape((layers, share_w, 2, total)),
            shape((layers, groups, width, cols)), shape((layers, width, 2, ff)),
        ),
        in_specs=[anywhere] * 6,
        out_specs=(anywhere,) * 6,
        scratch_shapes=[dma((8 + reps,))],
        compiler_params=pltpu.CompilerParams(vmem_limit_bytes=2**17),
    )(*outs)
    return (qm[None], qv[None], jnp.transpose(wm, (0, 2, 1, 3))[None], jnp.transpose(wv, (0, 2, 1, 3))[None],
            jnp.transpose(qt, (0, 2, 1, 3)), wt)


def solution(mesh):
    delta = P("rep", None, "shard", None, "tp")
    state = P("tp", None, None, ("rep", "shard"), None)
    train = P(None, "shard", None, "tp")
    return jax.shard_map(
        per_device, mesh=mesh, in_specs=(delta, delta, P(), state, state, state, state),
        out_specs=(state, state, state, state, train, train), check_vma=False,
    )
```
